32 devices in a mesh: cluster: 8 (over z, core), member: 4 (over y, x).
Axes of the slice: x: 2, y: 2, z: 4, core: 2. Of those that a mesh axis runs over, the one named last changes fastest.
Arguments:
- cam_jac: bfloat16 [18, 8, 16384], P(None, None, ('cluster', 'member')), may hold values from -0.625 to 0.625
- point_jac: bfloat16 [6, 8, 16384], P(None, None, ('cluster', 'member')), may hold values from -6 to 6
- residuals: bfloat16 [2, 8, 16384], P(None, None, ('cluster', 'member')), may hold values from -6 to 6
- obs_camera: int32 [8, 16384], P(None, ('cluster', 'member')), may hold values from 0 to 2047, as said below
- obs_count: int32 [16384], P(('cluster', 'member')), may hold values from 2 to 8, as said below
- new_cluster: int32 [2048], replicated, may hold values from 0 to 7, as said below
- new_slot: int32 [2048], replicated, may hold values from 0 to 255, as said below
Outputs:
- reduced_system: float32 [18432, 2304], P(('cluster', 'member'))
- camera_step: float32 [18432], P(('cluster', 'member'))
The draws below stay inside these ranges and needn't reach their ends.
Inputs may be any that keep to these rules, and one draw needn't show every extreme that they name: `obs_camera`: old ids: camera i lies in old cluster i // 256; a point block stored on the devices of cluster c observes cameras of old cluster c only, distinct ones in all its slots. Its live observations lie in new cluster c except at most two that lie in a single other new cluster. On every device, for each other cluster, at most 16 point blocks have live observations there, and exactly 16 for some other cluster. `obs_count`: some point block of every device has 8 live observations. `new_cluster`: each old cluster keeps all but 64 of its cameras; every new cluster holds exactly 256 cameras. `new_slot`: cameras of one new cluster have distinct rows.
All inputs are finite; a program needn't handle non-finite values.
Results may differ from the reference program's by a relative error of at most 0.0038.
Values may be sent and summed in bfloat16 or wider, within the bound.
A program may use at most 192 MiB of HBM per device.

```python
import jax
import jax.numpy as jnp
from jax import lax

SHOTS_EACH_BATCH = 256
PANEL = 16
OBS = 8
MOVE = 64
BCAP = 16
PT_DEV = 512
POINTS = 16384
N_CLUSTER = 8
N_MEMBER = 4


def viewpoint_arrangement(key):
    cluster_count = N_CLUSTER
    first_keys = jax.random.split(jax.random.fold_in(key, 101), cluster_count)
    tiebreak_keys = jax.random.split(jax.random.fold_in(key, 102), cluster_count)
    mixed_slot_number = jax.vmap(lambda iteration_tally: jax.random.permutation(iteration_tally, SHOTS_EACH_BATCH))(first_keys).astype(jnp.int32)
    relabel_batch_items = jax.vmap(lambda iteration_tally: jax.random.permutation(iteration_tally, SHOTS_EACH_BATCH))(tiebreak_keys).astype(jnp.int32)
    clusters = jnp.arange(cluster_count, dtype=jnp.int32)[:, None]
    moving = mixed_slot_number < MOVE
    aimed_batch = jnp.where(moving, (clusters + 1 + mixed_slot_number % (cluster_count - 1)) % cluster_count, clusters)
    renamed_measurements = relabel_batch_items[aimed_batch, mixed_slot_number]
    landmark_inverse_tiles = jnp.argsort(mixed_slot_number, axis=1).astype(jnp.int32)
    return (aimed_batch.astype(jnp.int32), renamed_measurements.astype(jnp.int32), landmark_inverse_tiles)


def observation_layout(key):
    cluster_count = N_CLUSTER
    device_count = N_CLUSTER * N_MEMBER
    aimed_batch, renamed_measurements, landmark_inverse_tiles = viewpoint_arrangement(key)
    point_key = jax.random.fold_in(key, 103)
    device_ids = jnp.arange(device_count, dtype=jnp.int32)

    def one_device(device):
        device_key = jax.random.fold_in(point_key, device)
        home_cluster = device // N_MEMBER
        device_keys = jax.random.split(device_key, 7)
        group_loads = jax.random.randint(device_keys[0], (cluster_count - 1,), max(1, BCAP // 4), BCAP + 1)
        fullest = jax.random.randint(device_keys[1], (), 0, cluster_count - 1)
        group_loads = jnp.where(jnp.arange(cluster_count - 1) == fullest, BCAP, group_loads)
        padded_loads = jnp.concatenate([group_loads, jnp.zeros((1,), jnp.int32)])
        shuffled = jax.random.permutation(device_keys[2], PT_DEV).astype(jnp.int32)
        group_index = jnp.minimum(shuffled // BCAP, cluster_count - 1)
        within = shuffled % BCAP
        boundary = (group_index < cluster_count - 1) & (within < padded_loads[group_index])
        counts = jax.random.randint(device_keys[3], (PT_DEV,), 2, OBS + 1)
        counts = counts.at[0].set(OBS)
        movers = jnp.where(counts >= 3, jax.random.randint(device_keys[4], (PT_DEV,), 1, 3), 1)
        remaining_labels = jax.random.split(device_keys[5], PT_DEV)
        stayers = jax.vmap(lambda iteration_tally: jax.random.permutation(iteration_tally, SHOTS_EACH_BATCH - MOVE)[:OBS])(remaining_labels).astype(jnp.int32) + MOVE
        per_group = jnp.maximum((MOVE - group_index + cluster_count - 2) // (cluster_count - 1), 2)
        random_ints = jax.random.randint(device_keys[6], (PT_DEV, 4), 0, 1 << 20)
        first_pick = random_ints[:, 0] % per_group
        second_pick = (first_pick + 1 + random_ints[:, 1] % (per_group - 1)) % per_group
        first_spot = random_ints[:, 2] % counts
        second_spot = (first_spot + 1 + random_ints[:, 3] % (counts - 1)) % counts
        first_rank = group_index + (cluster_count - 1) * first_pick
        second_rank = group_index + (cluster_count - 1) * second_pick
        slot_index = jnp.arange(OBS, dtype=jnp.int32)[None, :]
        use_first = boundary[:, None] & (slot_index == first_spot[:, None])
        use_second = boundary[:, None] & (movers[:, None] == 2) & (slot_index == second_spot[:, None])
        chosen = jnp.where(use_first, first_rank[:, None], jnp.where(use_second, second_rank[:, None], stayers))
        local_ids = landmark_inverse_tiles[home_cluster][chosen]
        return ((home_cluster * SHOTS_EACH_BATCH + local_ids).T.astype(jnp.int32), counts.astype(jnp.int32))
    cameras, counts = jax.vmap(one_device)(device_ids)
    return (cameras.transpose(1, 0, 2).reshape(OBS, device_count * PT_DEV), counts.reshape(-1))


def draw_obs_camera(key, part):
    return observation_layout(key)[0]


def draw_obs_count(key, part):
    return observation_layout(key)[1]


def draw_new_cluster(key, part):
    return viewpoint_arrangement(key)[0].reshape(-1)


def draw_new_slot(key, part):
    return viewpoint_arrangement(key)[1].reshape(-1)


def block_levels(stream_key, shape, shards, smallest, top_value):
    loudness = 1.0
    for dim, shards_of in shards:
        heights = jax.random.uniform(jax.random.fold_in(jax.random.fold_in(stream_key, 6), dim), (shards_of,), jnp.float32, smallest / len(shards), top_value / len(shards))
        loudness = loudness * jnp.repeat(jnp.exp(heights), shape[dim] // shards_of).reshape((-1,) + (1,) * (len(shape) - 1 - dim))
    return loudness


def normal_values(rng, dims, spread, reach, cuts=(), held_as=jnp.bfloat16):
    values = jax.random.normal(rng, dims, jnp.float32) * spread
    if len(cuts) > 0:
        values = block_levels(rng, dims, cuts, -0.22, 0.18) * values
    return jnp.clip(values, min=-reach, max=reach).astype(held_as)


def setup_inputs(seed: int = 0) -> dict:
    splits = jax.random.split(jax.random.key(seed), 8)
    return {
        "cam_jac": normal_values(splits[0], (18, OBS, POINTS), (10 * PT_DEV * N_MEMBER // SHOTS_EACH_BATCH) ** -0.5, 0.625, ((2, 32),)),
        "point_jac": normal_values(splits[1], (6, OBS, POINTS), 1.0, 6.0, ((2, 32),)),
        "residuals": normal_values(splits[2], (2, OBS, POINTS), 1.0, 6.0, ((2, 32),)),
        "obs_camera": draw_obs_camera(jax.random.fold_in(splits[7], 71), 0),
        "obs_count": draw_obs_count(jax.random.fold_in(splits[7], 71), 0),
        "new_cluster": draw_new_cluster(jax.random.fold_in(splits[7], 71), 0),
        "new_slot": draw_new_slot(jax.random.fold_in(splits[7], 71), 0),
    }


DAMPING = 0.5
EXACT_PRECISION = lax.Precision.HIGHEST

def invert_three(matrix):

    def cofactor(i, j):
        keep_rows = [r for r in range(3) if r != i]
        keep_cols = [r for r in range(3) if r != j]
        minor_value = matrix[keep_rows[0], keep_cols[0]] * matrix[keep_rows[1], keep_cols[1]] - matrix[keep_rows[0], keep_cols[1]] * matrix[keep_rows[1], keep_cols[0]]
        sign_value = 1.0 if (i + j) % 2 == 0 else -1.0
        return sign_value * minor_value
    cofactors = [[cofactor(i, j) for j in range(3)] for i in range(3)]
    determinant = matrix[0, 0] * cofactors[0][0] + matrix[0, 1] * cofactors[0][1] + matrix[0, 2] * cofactors[0][2]
    adjugate = jnp.stack([jnp.stack([cofactors[j][i] for j in range(3)]) for i in range(3)])
    return adjugate / determinant

def eliminate(cam_part, point_part, resid_part, slot_rows):
    valid_mask = (slot_rows >= 0).astype(jnp.float32)
    obs_slots = slot_rows.shape[0]
    block_count = slot_rows.shape[1]
    camera_rows = (cam_part.astype(jnp.float32) * valid_mask).reshape(2, 9, obs_slots, block_count)
    point_rows = (point_part.astype(jnp.float32) * valid_mask).reshape(2, 3, obs_slots, block_count)
    resid_rows = resid_part.astype(jnp.float32) * valid_mask
    normal_point = jnp.einsum('kbon,kcon->bcn', point_rows, point_rows, precision=EXACT_PRECISION) + DAMPING * jnp.eye(3, dtype=jnp.float32)[:, :, None]
    point_grad = jnp.einsum('kbon,kon->bn', point_rows, resid_rows, precision=EXACT_PRECISION)
    landmark_inverse_tiles = invert_three(normal_point)
    camera_point_coupling = jnp.einsum('kaon,kbon->abon', camera_rows, point_rows, precision=EXACT_PRECISION).astype(jnp.bfloat16)
    reduced_camera_matrix = jnp.einsum('wrsd,rpd->wpsd', camera_point_coupling.astype(jnp.float32), landmark_inverse_tiles, precision=EXACT_PRECISION).astype(jnp.bfloat16)
    camera_normal = jnp.einsum('kaon,kcon->acon', camera_rows, camera_rows, precision=EXACT_PRECISION)
    camera_grad = jnp.einsum('kaon,kon->aon', camera_rows, resid_rows, precision=EXACT_PRECISION) - jnp.einsum('abon,bn->aon', reduced_camera_matrix.astype(jnp.float32), point_grad, precision=EXACT_PRECISION)
    camera_terms = jnp.concatenate([camera_normal.reshape(81, obs_slots, block_count), camera_grad], axis=0)
    return (camera_point_coupling, reduced_camera_matrix, camera_terms)

def reference(cam_jac, point_jac, residuals, obs_camera, obs_count, new_cluster, new_slot):
    total_points = obs_camera.shape[1]
    block_total = total_points // PT_DEV
    live_mask = lax.broadcasted_iota(jnp.int32, obs_camera.shape, 0) < obs_count[None, :]
    cluster_of = jnp.take(new_cluster, obs_camera)
    row_of = jnp.take(new_slot, obs_camera)

    def blocked(array):
        shaped = array.reshape(array.shape[:-1] + (block_total, PT_DEV))
        return jnp.moveaxis(shaped, -2, 0)
    cam_blocks = blocked(cam_jac)
    point_blocks = blocked(point_jac)
    resid_blocks = blocked(residuals)
    panel_width = 9 * PANEL
    panel_total = SHOTS_EACH_BATCH // PANEL
    system_list = []
    solved_step_list = []
    for cluster in range(N_CLUSTER):
        slot_rows = jnp.where(live_mask & (cluster_of == cluster), row_of, -1).astype(jnp.int32)
        slot_blocks = blocked(slot_rows)

        def accumulate(carry_pair, block_items):
            flat_sum, camera_total = carry_pair
            cam_part, point_part, resid_part, slot_part = block_items
            camera_point_coupling, reduced_camera_matrix, camera_terms = eliminate(cam_part, point_part, resid_part, slot_part)
            pair_blocks = jnp.einsum('abjn,cbkn->njkac', reduced_camera_matrix.astype(jnp.float32), camera_point_coupling.astype(jnp.float32), precision=EXACT_PRECISION)
            safe_ids = jnp.where(slot_part < 0, SHOTS_EACH_BATCH, slot_part).astype(jnp.int32)
            id_rows = safe_ids.T
            flat_index = (id_rows[:, :, None] * (SHOTS_EACH_BATCH + 1) + id_rows[:, None, :]).reshape(-1)
            flat_sum = flat_sum.at[flat_index].add(pair_blocks.reshape(-1, 9, 9))
            per_camera = jax.ops.segment_sum(camera_terms.reshape(90, -1).T, safe_ids.reshape(-1), num_segments=SHOTS_EACH_BATCH + 1)
            camera_total = camera_total + per_camera[:SHOTS_EACH_BATCH].T
            return ((flat_sum, camera_total), None)
        start_state = (jnp.zeros(((SHOTS_EACH_BATCH + 1) * (SHOTS_EACH_BATCH + 1), 9, 9), jnp.float32), jnp.zeros((90, SHOTS_EACH_BATCH), jnp.float32))
        (flat_sum, camera_total), _ = lax.scan(accumulate, start_state, (cam_blocks, point_blocks, resid_blocks, slot_blocks))
        pair_total = flat_sum.reshape(SHOTS_EACH_BATCH + 1, SHOTS_EACH_BATCH + 1, 9, 9)[:SHOTS_EACH_BATCH, :SHOTS_EACH_BATCH].transpose(0, 2, 1, 3).reshape(9 * SHOTS_EACH_BATCH, 9 * SHOTS_EACH_BATCH)
        normal_blocks = camera_total[:81].reshape(9, 9, SHOTS_EACH_BATCH) + DAMPING * jnp.eye(9, dtype=jnp.float32)[:, :, None]
        identity_cams = jnp.eye(SHOTS_EACH_BATCH, dtype=jnp.float32)
        block_diag = (normal_blocks.transpose(2, 0, 1)[:, :, None, :] * identity_cams[:, None, :, None]).reshape(9 * SHOTS_EACH_BATCH, 9 * SHOTS_EACH_BATCH)
        reduced_matrix = block_diag - pair_total
        gradient = camera_total[81:].T.reshape(-1)
        diagonal = jnp.stack([reduced_matrix[q * panel_width:(q + 1) * panel_width, q * panel_width:(q + 1) * panel_width] for q in range(panel_total)])
        factor = jnp.linalg.cholesky(diagonal)
        solved = jax.scipy.linalg.cho_solve((factor, True), gradient.reshape(panel_total, panel_width)[..., None])[..., 0]
        system_list.append(reduced_matrix)
        solved_step_list.append(-solved.reshape(-1))
    return (jnp.concatenate(system_list, axis=0), jnp.concatenate(solved_step_list, axis=0))
```

```python
import functools

import jax
import jax.numpy as jnp
import numpy as np
from jax import lax
from jax.experimental import pallas as pl
from jax.experimental.pallas import tpu as pltpu
from jax.sharding import PartitionSpec as P

SHOTS = 256
PANEL = 16
BCAP = 16
DAMPING = 0.5
ROWS = 28
PW = 9 * PANEL
BF = jnp.bfloat16
F32 = jnp.float32
NT = (((1,), (1,)), ((), ()))


def pack_kernel(me_ref, table_ref, cam_ref, point_ref, resid_ref, ids_ref, count_ref,
                home_ref, far_ref, payload, *, clusters, width):
    me = me_ref[0]
    obs, points = ids_ref.shape
    ids = ids_ref[...] - me * SHOTS
    table = table_ref[...]
    camera = lax.broadcasted_iota(jnp.int32, (SHOTS, points), 0)
    codes = [
        jnp.sum(jnp.where(camera == ids[o : o + 1], table, 0.0), axis=0, keepdims=True)
        for o in range(obs)
    ]
    code = jnp.concatenate(codes, axis=0).astype(jnp.int32)
    cluster = code // SHOTS
    row = code - cluster * SHOTS
    live = lax.broadcasted_iota(jnp.int32, (obs, points), 0) < count_ref[...]
    home = live & (cluster == me)
    abroad = live & (cluster != me)
    home_f = home.astype(F32)
    slot_f = jnp.where(home, row + 1, 0).astype(F32)
    for j in range(points // width):
        cols = slice(j * width, (j + 1) * width)
        for k in range(18):
            home_ref[j, k] = (cam_ref[k, :, cols].astype(F32) * home_f[:, cols]).astype(BF)
        for k in range(6):
            home_ref[j, 18 + k] = (point_ref[k, :, cols].astype(F32) * home_f[:, cols]).astype(BF)
        for k in range(2):
            home_ref[j, 24 + k] = (resid_ref[k, :, cols].astype(F32) * home_f[:, cols]).astype(BF)
        home_ref[j, 26] = slot_f[:, cols].astype(BF)
        home_ref[j, 27] = jnp.zeros((obs, width), BF)
    aimed = jnp.max(jnp.where(abroad, cluster, -1), axis=0, keepdims=True)
    hits = (aimed == lax.broadcasted_iota(jnp.int32, (clusters, points), 0)).astype(F32)
    before = (
        lax.broadcasted_iota(jnp.int32, (points, points), 0)
        < lax.broadcasted_iota(jnp.int32, (points, points), 1)
    ).astype(BF)
    rank = jnp.sum(
        jnp.dot(hits.astype(BF), before, preferred_element_type=F32) * hits, axis=0, keepdims=True
    ).astype(jnp.int32)
    column = jnp.where(aimed >= 0, aimed * BCAP + rank, -1)
    chooser = (
        lax.broadcasted_iota(jnp.int32, (clusters * BCAP, points), 0) == column
    ).astype(BF)
    seen = jnp.zeros((1, points), F32)
    abroad_f = abroad.astype(F32)
    firsts = []
    for o in range(obs):
        here = abroad_f[o : o + 1]
        firsts.append(jnp.where(seen == 0, here, 0.0))
        seen = seen + here
    first = jnp.concatenate(firsts, axis=0)
    second = abroad_f - first
    payload[...] = jnp.zeros_like(payload)
    for r, mask in enumerate((first, second)):
        for k in range(18):
            payload[r * 32 + k : r * 32 + k + 1, :] = jnp.sum(
                cam_ref[k].astype(F32) * mask, axis=0, keepdims=True
            )
        for k in range(6):
            payload[r * 32 + 18 + k : r * 32 + 19 + k, :] = jnp.sum(
                point_ref[k].astype(F32) * mask, axis=0, keepdims=True
            )
        for k in range(2):
            payload[r * 32 + 24 + k : r * 32 + 25 + k, :] = jnp.sum(
                resid_ref[k].astype(F32) * mask, axis=0, keepdims=True
            )
        payload[r * 32 + 26 : r * 32 + 27, :] = jnp.sum(
            (row + 1).astype(F32) * mask, axis=0, keepdims=True
        )
    far_ref[...] = lax.dot_general(
        chooser, payload[...].astype(BF), NT, preferred_element_type=F32
    ).astype(BF)


def main_kernel(first_ref, g_ref, tab_ref, pick_ref, damp_ref, rowcam_ref, colcam_ref,
                out_ref, step_ref, tw, tz, terms, sw, sz, sb, wp, zp, accu, ut, gt, dacc, *, share):
    t = pl.program_id(0)
    first = first_ref[0]
    first_panel = first // PANEL
    panels = share // PANEL
    rows = 9 * share
    obs, n = g_ref.shape[2], g_ref.shape[3]
    columns = out_ref.shape[1]

    @pl.when(t == 0)
    def _():
        terms[...] = jnp.zeros_like(terms)
        accu[...] = jnp.zeros_like(accu)
        dacc[...] = jnp.zeros_like(dacc)
        out_ref[...] = jnp.zeros_like(out_ref)

    x = lambda k: g_ref[0, k].astype(F32)
    A = [[x(k * 9 + a) for a in range(9)] for k in range(2)]
    B = [[x(18 + k * 3 + b) for b in range(3)] for k in range(2)]
    e = [x(24 + k) for k in range(2)]
    slot = x(26) - 1.0
    total = lambda u: jnp.sum(u, axis=0, keepdims=True)
    V = [[None] * 3 for _ in range(3)]
    for b in range(3):
        for c in range(b, 3):
            v = total(B[0][b] * B[0][c] + B[1][b] * B[1][c])
            V[b][c] = V[c][b] = v + DAMPING if b == c else v
    g = [total(B[0][b] * e[0] + B[1][b] * e[1]) for b in range(3)]

    def cofactor(i, j):
        r = [u for u in range(3) if u != i]
        c = [u for u in range(3) if u != j]
        m = V[r[0]][c[0]] * V[r[1]][c[1]] - V[r[0]][c[1]] * V[r[1]][c[0]]
        return m if (i + j) % 2 == 0 else -m

    cof = [[cofactor(i, j) for j in range(3)] for i in range(3)]
    det = V[0][0] * cof[0][0] + V[0][1] * cof[0][1] + V[0][2] * cof[0][2]
    inv = [[jnp.broadcast_to(cof[j][i] / det, (obs, n)) for j in range(3)] for i in range(3)]
    g = [jnp.broadcast_to(u, (obs, n)) for u in g]

    def keep(index, u):
        for h in range(n // 128):
            terms[h, index * obs : (index + 1) * obs, :] = u[:, h * 128 : (h + 1) * 128]

    for a in range(9):
        W = [
            (A[0][a] * B[0][b] + A[1][a] * B[1][b]).astype(BF).astype(F32) for b in range(3)
        ]
        Z = [
            (W[0] * inv[0][b] + W[1] * inv[1][b] + W[2] * inv[2][b]).astype(BF).astype(F32)
            for b in range(3)
        ]
        for b in range(3):
            for r in range(a, 24, 9):
                for h in range(n // 128):
                    lanes = slice(h * 128, (h + 1) * 128)
                    tw[h * 3 + b, r * obs : (r + 1) * obs, :] = W[b][:, lanes]
                    tz[h * 3 + b, r * obs : (r + 1) * obs, :] = Z[b][:, lanes]
        for c in range(a, 9):
            u = A[0][a] * A[0][c] + A[1][a] * A[1][c]
            keep(a * 9 + c, u)
            if c != a:
                keep(c * 9 + a, u)
        keep(81 + a, A[0][a] * e[0] + A[1][a] * e[1] - (Z[0] * g[0] + Z[1] * g[1] + Z[2] * g[2]))

    own = lax.broadcasted_iota(jnp.int32, (share, n), 0).astype(F32) + first.astype(F32)
    added = jnp.zeros((share, 128), F32)
    for o in range(obs):
        onehot = (jnp.broadcast_to(slot[o : o + 1], (share, n)) == own).astype(F32).astype(BF)
        u = jnp.concatenate(
            [terms[h, pl.ds(o, 128, stride=obs), :] for h in range(n // 128)],
            axis=1,
        )
        high = u.astype(BF)
        low = (u - high.astype(F32)).astype(BF)
        added += lax.dot_general(onehot, high, NT, preferred_element_type=F32)
        added += lax.dot_general(onehot, low, NT, preferred_element_type=F32)
        sb[o] = jnp.broadcast_to(slot[o : o + 1], (16, n)).astype(BF)
    accu[...] += added

    for o in range(obs):
        for b in range(3):
            for v in range(9):
                start = ((16 * v) % 9) * obs + o
                for h in range(n // 128):
                    lanes = slice(h * 128, (h + 1) * 128)
                    sw[o * 3 + b, v * 16 : (v + 1) * 16, lanes] = tw[
                        h * 3 + b, pl.ds(start, 16, stride=obs), :
                    ].astype(BF)
                    sz[o * 3 + b, v * 16 : (v + 1) * 16, lanes] = tz[
                        h * 3 + b, pl.ds(start, 16, stride=obs), :
                    ].astype(BF)

    def place(source, target, index, panel):
        shift = (panel * PANEL).astype(F32).astype(BF)
        base = pl.multiple_of(index * PW, PW)
        for h in range(n // 128):
            lanes = slice(h * 128, (h + 1) * 128)
            acc = [[jnp.zeros((16, 128), BF) for _ in range(9)] for _ in range(3)]
            for o in range(obs):
                s = sb[o, :, lanes] - shift
                for v in range(9):
                    hit = s == tab_ref[v * 16 : (v + 1) * 16, :]
                    for b in range(3):
                        acc[b][v] = jnp.where(
                            hit, source[o * 3 + b, v * 16 : (v + 1) * 16, lanes], acc[b][v]
                        )
            for b in range(3):
                for v in range(9):
                    target[
                        pl.ds(base + v * 16, 16), b * n + h * 128 : b * n + (h + 1) * 128
                    ] = acc[b][v]

    def place_w(i, c):
        place(sw, wp, i, i)
        return c

    def place_z(i, c):
        place(sz, zp, i, i + first_panel)
        return c

    lax.fori_loop(0, SHOTS // PANEL, place_w, 0)
    lax.fori_loop(0, panels, place_z, 0)

    def multiply(j, c):
        at = pl.ds(pl.multiple_of(j * 256, 256), 256)
        out_ref[:, at] += lax.dot_general(zp[...], wp[at, :], NT, preferred_element_type=F32)
        return c

    lax.fori_loop(0, columns // 256, multiply, 0)

    def multiply_own(q, c):
        at = pl.ds(pl.multiple_of(q * PW, PW), PW)
        dacc[at, 0:PW] += lax.dot_general(
            zp[at, :],
            wp[pl.ds(pl.multiple_of((q + first_panel) * PW, PW), PW), :],
            NT,
            preferred_element_type=F32,
        )
        return c

    lax.fori_loop(0, panels, multiply_own, 0)

    @pl.when(t == pl.num_programs(0) - 1)
    def _():
        acc = accu[...]
        for a in range(9):
            ut[pl.ds(a, share, stride=9), :] = acc if a == 0 else pltpu.roll(acc, 128 - 9 * a, 1)
            gt[pl.ds(a, share, stride=9), :] = pltpu.roll(acc, 128 - 81 - a, 1)
        u = ut[...] + damp_ref[...]
        high = u.astype(BF)
        low = (u - high.astype(F32)).astype(BF)
        rowcam = rowcam_ref[:, 0:1]

        def blocks(pick):
            return jnp.dot(high, pick, preferred_element_type=F32) + jnp.dot(
                low, pick, preferred_element_type=F32
            )

        def finish(j, c):
            at = pl.ds(pl.multiple_of(j * 256, 256), 256)
            hit = rowcam + first.astype(F32) == colcam_ref[0:1, at]
            out_ref[:, at] = jnp.where(hit, blocks(pick_ref[:, at]), 0.0) - out_ref[:, at]
            return c

        lax.fori_loop(0, columns // 256, finish, 0)
        local = rowcam_ref[:, 1:2]
        lane = lax.broadcasted_iota(jnp.int32, (rows, 256), 1)
        m = jnp.where(local == colcam_ref[0:1, 0:256], blocks(pick_ref[:, 0:256]), 0.0) - dacc[...]
        dacc[...] = jnp.where(lane == PW, gt[:, 0:1], m)

        def eliminate(half, k, c):
            for q in range(panels):
                at = slice(q * PW, (q + 1) * PW)
                ids = lax.broadcasted_iota(jnp.int32, (PW, 128), 1) + half * 128
                col = jnp.sum(
                    jnp.where(ids == k, dacc[at, half * 128 : (half + 1) * 128], 0.0),
                    axis=1,
                    keepdims=True,
                )
                pivot = dacc[pl.ds(q * PW + k, 1), :]
                wide = lax.broadcasted_iota(jnp.int32, (1, 256), 1)
                p = jnp.sum(jnp.where(wide == k, pivot, 0.0), axis=1, keepdims=True)
                scaled = pivot / p
                down = lax.broadcasted_iota(jnp.int32, (PW, 1), 0)
                col = jnp.where(down == k, 0.0, col)
                dacc[at, :] = dacc[at, :] - col * scaled
            return c

        lax.fori_loop(0, 128, functools.partial(eliminate, 0), 0)
        lax.fori_loop(128, PW, functools.partial(eliminate, 1), 0)
        for q in range(panels):
            at = slice(q * PW, (q + 1) * PW)
            m = dacc[at, :]
            down = lax.broadcasted_iota(jnp.int32, (PW, 256), 0)
            across = lax.broadcasted_iota(jnp.int32, (PW, 256), 1)
            diag = jnp.sum(jnp.where(down == across, m, 0.0), axis=1, keepdims=True)
            rhs = jnp.sum(jnp.where(across == PW, m, 0.0), axis=1, keepdims=True)
            step_ref[at, :] = jnp.broadcast_to(-(rhs / diag), (PW, 128))


def per_device(cam_jac, point_jac, residuals, obs_camera, obs_count, new_cluster, new_slot):
    clusters = lax.axis_size("cluster")
    members = lax.axis_size("member")
    me = lax.axis_index("cluster").astype(jnp.int32)
    my_member = lax.axis_index("member").astype(jnp.int32)
    obs, points = obs_camera.shape
    width = min(256, points)
    share = SHOTS // members
    rows = 9 * share
    columns = 9 * SHOTS
    vmem = pl.BlockSpec(memory_space=pltpu.VMEM)
    smem = pl.BlockSpec(memory_space=pltpu.SMEM)

    code = (new_cluster * SHOTS + new_slot).astype(F32)
    table = lax.dynamic_slice_in_dim(code, me * SHOTS, SHOTS, 0)[:, None]
    home, far = pl.pallas_call(
        functools.partial(pack_kernel, clusters=clusters, width=width),
        out_shape=(
            jax.ShapeDtypeStruct((points // width, ROWS, obs, width), BF),
            jax.ShapeDtypeStruct((clusters * BCAP, 64), BF),
        ),
        in_specs=[smem] + [vmem] * 6,
        out_specs=(vmem, vmem),
        scratch_shapes=[pltpu.VMEM((64, points), F32)],
        name="pack",
    )(me[None], table, cam_jac, point_jac, residuals, obs_camera, obs_count[None, :])

    far = jnp.broadcast_to(
        far.reshape(clusters, 1, BCAP, 64), (clusters, members, BCAP, 64)
    ).reshape(clusters * members, BCAP, 64)
    far = lax.all_to_all(far, ("cluster", "member"), split_axis=0, concat_axis=0, tiled=True)
    home = lax.all_to_all(
        jnp.broadcast_to(home[None], (members,) + home.shape),
        "member", split_axis=0, concat_axis=0, tiled=True,
    ).reshape(-1, ROWS, obs, width)
    far = far.reshape(-1, width, 2, 32)[:, :, :, :ROWS].transpose(0, 3, 2, 1)
    far = jnp.pad(far, ((0, 0), (0, 0), (0, obs - 2), (0, 0)))
    data = jnp.concatenate([home, far], axis=0)

    r = np.arange(rows)
    c = np.arange(columns)
    lane = np.arange(128)
    tab = jnp.asarray(np.broadcast_to((np.arange(PW) // 9)[:, None], (PW, 128)), BF)
    pick = jnp.asarray(lane[:, None] == c[None, :] % 9, BF)
    damp = jnp.asarray(DAMPING * (lane[None, :] == (r % 9)[:, None]), F32)
    rowcam = np.zeros((rows, 128), np.float32)
    rowcam[:, 0] = r // 9
    rowcam[:, 1] = (r // 9) % PANEL
    colcam = jnp.asarray(np.broadcast_to((c // 9)[None, :], (8, columns)), F32)
    full = lambda s: pl.BlockSpec(s, lambda t: (0,) * len(s))
    out, step = pl.pallas_call(
        functools.partial(main_kernel, share=share),
        grid=(data.shape[0],),
        out_shape=(
            jax.ShapeDtypeStruct((rows, columns), F32),
            jax.ShapeDtypeStruct((rows, 128), F32),
        ),
        in_specs=[
            smem,
            pl.BlockSpec((1, ROWS, obs, width), lambda t: (t, 0, 0, 0)),
            full((PW, 128)),
            full((128, columns)),
            full((rows, 128)),
            full((rows, 128)),
            full((8, columns)),
        ],
        out_specs=(full((rows, columns)), full((rows, 128))),
        scratch_shapes=[
            pltpu.VMEM((width // 128 * 3, 24 * obs, 128), F32),
            pltpu.VMEM((width // 128 * 3, 24 * obs, 128), F32),
            pltpu.VMEM((width // 128, 128 * obs, 128), F32),
            pltpu.VMEM((3 * obs, PW, width), BF),
            pltpu.VMEM((3 * obs, PW, width), BF),
            pltpu.VMEM((obs, 16, width), BF),
            pltpu.VMEM((columns, 3 * width), BF),
            pltpu.VMEM((rows, 3 * width), BF),
            pltpu.VMEM((share, 128), F32),
            pltpu.VMEM((rows, 128), F32),
            pltpu.VMEM((rows, 128), F32),
            pltpu.VMEM((rows, 256), F32),
        ],
        compiler_params=pltpu.CompilerParams(vmem_limit_bytes=56 * 1024 * 1024),
        name="schur",
    )((my_member * share)[None], data, tab, pick, damp, jnp.asarray(rowcam), colcam)
    return (out, step[:, 0])


def solution(mesh):
    in_specs = (
        P(None, None, ("cluster", "member")),
        P(None, None, ("cluster", "member")),
        P(None, None, ("cluster", "member")),
        P(None, ("cluster", "member")),
        P(("cluster", "member")),
        P(),
        P(),
    )
    out_specs = (P(("cluster", "member"), None), P(("cluster", "member")))
    return jax.shard_map(
        per_device, mesh=mesh, in_specs=in_specs, out_specs=out_specs, check_vma=False
    )
```

```python
import functools

import jax
import jax.numpy as jnp
import numpy as np
from jax import lax
from jax.experimental import pallas as pl
from jax.experimental.pallas import tpu as pltpu
from jax.sharding import PartitionSpec as P

SHOTS = 256
PANEL = 16
BCAP = 16
DAMPING = 0.5
ROWS = 28
PW = 9 * PANEL
BF = jnp.bfloat16
F32 = jnp.float32
NT = (((1,), (1,)), ((), ()))


def pack_kernel(me_ref, table_ref, cam_ref, point_ref, resid_ref, ids_ref, count_ref,
                home_ref, far_ref, payload, *, clusters, width):
    me = me_ref[0]
    obs, points = ids_ref.shape
    ids = ids_ref[...] - me * SHOTS
    table = table_ref[...]
    camera = lax.broadcasted_iota(jnp.int32, (SHOTS, points), 0)
    codes = [
        jnp.sum(jnp.where(camera == ids[o : o + 1], table, 0.0), axis=0, keepdims=True)
        for o in range(obs)
    ]
    code = jnp.concatenate(codes, axis=0).astype(jnp.int32)
    cluster = code // SHOTS
    row = code - cluster * SHOTS
    live = lax.broadcasted_iota(jnp.int32, (obs, points), 0) < count_ref[...]
    home = live & (cluster == me)
    abroad = live & (cluster != me)
    home_f = home.astype(F32)
    slot_f = jnp.where(home, row + 1, 0).astype(F32)
    for j in range(points // width):
        cols = slice(j * width, (j + 1) * width)
        for k in range(18):
            home_ref[j, k] = (cam_ref[k, :, cols].astype(F32) * home_f[:, cols]).astype(BF)
        for k in range(6):
            home_ref[j, 18 + k] = (point_ref[k, :, cols].astype(F32) * home_f[:, cols]).astype(BF)
        for k in range(2):
            home_ref[j, 24 + k] = (resid_ref[k, :, cols].astype(F32) * home_f[:, cols]).astype(BF)
        home_ref[j, 26] = slot_f[:, cols].astype(BF)
        home_ref[j, 27] = jnp.zeros((obs, width), BF)
    aimed = jnp.max(jnp.where(abroad, cluster, -1), axis=0, keepdims=True)
    hits = (aimed == lax.broadcasted_iota(jnp.int32, (clusters, points), 0)).astype(F32)
    before = (
        lax.broadcasted_iota(jnp.int32, (points, points), 0)
        < lax.broadcasted_iota(jnp.int32, (points, points), 1)
    ).astype(BF)
    rank = jnp.sum(
        jnp.dot(hits.astype(BF), before, preferred_element_type=F32) * hits, axis=0, keepdims=True
    ).astype(jnp.int32)
    column = jnp.where(aimed >= 0, aimed * BCAP + rank, -1)
    chooser = (
        lax.broadcasted_iota(jnp.int32, (clusters * BCAP, points), 0) == column
    ).astype(BF)
    seen = jnp.zeros((1, points), F32)
    abroad_f = abroad.astype(F32)
    firsts = []
    for o in range(obs):
        here = abroad_f[o : o + 1]
        firsts.append(jnp.where(seen == 0, here, 0.0))
        seen = seen + here
    first = jnp.concatenate(firsts, axis=0)
    second = abroad_f - first
    payload[...] = jnp.zeros_like(payload)
    for r, mask in enumerate((first, second)):
        for k in range(18):
            payload[r * 32 + k : r * 32 + k + 1, :] = jnp.sum(
                cam_ref[k].astype(F32) * mask, axis=0, keepdims=True
            )
        for k in range(6):
            payload[r * 32 + 18 + k : r * 32 + 19 + k, :] = jnp.sum(
                point_ref[k].astype(F32) * mask, axis=0, keepdims=True
            )
        for k in range(2):
            payload[r * 32 + 24 + k : r * 32 + 25 + k, :] = jnp.sum(
                resid_ref[k].astype(F32) * mask, axis=0, keepdims=True
            )
        payload[r * 32 + 26 : r * 32 + 27, :] = jnp.sum(
            (row + 1).astype(F32) * mask, axis=0, keepdims=True
        )
    far_ref[...] = lax.dot_general(
        chooser, payload[...].astype(BF), NT, preferred_element_type=F32
    ).astype(BF)


def main_kernel(first_ref, g_ref, tab_ref, pick_ref, damp_ref, rowcam_ref, colcam_ref,
                out_ref, step_ref, tw, tz, terms, sw, sz, sb, wp, zp, accu, ut, gt, dacc, *, share, home_steps):
    t = pl.program_id(0)
    first = first_ref[0]
    first_panel = first // PANEL
    panels = share // PANEL
    rows = 9 * share
    obs, n = g_ref.shape[2], g_ref.shape[3]
    columns = out_ref.shape[1]

    @pl.when(t == 0)
    def _():
        terms[...] = jnp.zeros_like(terms)
        accu[...] = jnp.zeros_like(accu)
        dacc[...] = jnp.zeros_like(dacc)
        out_ref[...] = jnp.zeros_like(out_ref)

    x = lambda k: g_ref[0, k].astype(F32)
    A = [[x(k * 9 + a) for a in range(9)] for k in range(2)]
    B = [[x(18 + k * 3 + b) for b in range(3)] for k in range(2)]
    e = [x(24 + k) for k in range(2)]
    slot = x(26) - 1.0
    total = lambda u: jnp.sum(u, axis=0, keepdims=True)
    V = [[None] * 3 for _ in range(3)]
    for b in range(3):
        for c in range(b, 3):
            v = total(B[0][b] * B[0][c] + B[1][b] * B[1][c])
            V[b][c] = V[c][b] = v + DAMPING if b == c else v
    g = [total(B[0][b] * e[0] + B[1][b] * e[1]) for b in range(3)]

    def cofactor(i, j):
        r = [u for u in range(3) if u != i]
        c = [u for u in range(3) if u != j]
        m = V[r[0]][c[0]] * V[r[1]][c[1]] - V[r[0]][c[1]] * V[r[1]][c[0]]
        return m if (i + j) % 2 == 0 else -m

    cof = [[cofactor(i, j) for j in range(3)] for i in range(3)]
    det = V[0][0] * cof[0][0] + V[0][1] * cof[0][1] + V[0][2] * cof[0][2]
    inv = [[jnp.broadcast_to(cof[j][i] / det, (obs, n)) for j in range(3)] for i in range(3)]
    g = [jnp.broadcast_to(u, (obs, n)) for u in g]

    def keep(index, u):
        for h in range(n // 128):
            terms[h, index * obs : (index + 1) * obs, :] = u[:, h * 128 : (h + 1) * 128]

    for a in range(9):
        W = [
            (A[0][a] * B[0][b] + A[1][a] * B[1][b]).astype(BF).astype(F32) for b in range(3)
        ]
        Z = [
            (W[0] * inv[0][b] + W[1] * inv[1][b] + W[2] * inv[2][b]).astype(BF).astype(F32)
            for b in range(3)
        ]
        for b in range(3):
            for r in range(a, 24, 9):
                for h in range(n // 128):
                    lanes = slice(h * 128, (h + 1) * 128)
                    tw[h * 3 + b, r * obs : (r + 1) * obs, :] = W[b][:, lanes]
                    tz[h * 3 + b, r * obs : (r + 1) * obs, :] = Z[b][:, lanes]
        for c in range(a, 9):
            u = A[0][a] * A[0][c] + A[1][a] * A[1][c]
            keep(a * 9 + c, u)
            if c != a:
                keep(c * 9 + a, u)
        keep(81 + a, A[0][a] * e[0] + A[1][a] * e[1] - (Z[0] * g[0] + Z[1] * g[1] + Z[2] * g[2]))

    own = lax.broadcasted_iota(jnp.int32, (share, n), 0).astype(F32) + first.astype(F32)
    added = jnp.zeros((share, 128), F32)
    for o in range(obs):
        onehot = (jnp.broadcast_to(slot[o : o + 1], (share, n)) == own).astype(F32).astype(BF)
        u = jnp.concatenate(
            [terms[h, pl.ds(o, 128, stride=obs), :] for h in range(n // 128)],
            axis=1,
        )
        high = u.astype(BF)
        low = (u - high.astype(F32)).astype(BF)
        added += lax.dot_general(onehot, high, NT, preferred_element_type=F32)
        added += lax.dot_general(onehot, low, NT, preferred_element_type=F32)
        for h in range(n // 128):
            sb[h * obs + o] = jnp.broadcast_to(
                slot[o : o + 1, h * 128 : (h + 1) * 128], (16, 128)
            ).astype(BF)
    accu[...] += added

    def place_one(source, target, index, panel):
        shift = (panel * PANEL).astype(F32).astype(BF)
        base = pl.multiple_of(index * PW, PW)
        for h in range(n // 128):
            lanes = slice(h * 128, (h + 1) * 128)
            acc = [[jnp.zeros((16, 128), BF) for _ in range(9)] for _ in range(3)]
            for o in range(obs):
                s = sb[h * obs + o] - shift
                for v in range(9):
                    hit = s == tab_ref[v * 16 : (v + 1) * 16, :]
                    for b in range(3):
                        acc[b][v] = jnp.where(
                            hit, source[h * 3 * obs + o * 3 + b, v * 16 : (v + 1) * 16, :], acc[b][v]
                        )
            for b in range(3):
                for v in range(9):
                    target[
                        pl.ds(base + v * 16, 16), b * n + h * 128 : b * n + (h + 1) * 128
                    ] = acc[b][v]

    def place(source, target, index, panel, group, used):
        base = pl.multiple_of(index * PW, PW)
        for h in range(n // 128):
            for v in range(9):
                tab = tab_ref[v * 16 : (v + 1) * 16, :]
                tabs = [tab + ((panel + u) * PANEL).astype(F32).astype(BF) for u in range(group)]
                acc = [[jnp.zeros((16, 128), BF) for _ in range(3)] for _ in range(group)]
                for o in range(used):
                    s = sb[h * obs + o]
                    values = [
                        source[h * 3 * obs + o * 3 + b, v * 16 : (v + 1) * 16, :] for b in range(3)
                    ]
                    for u in range(group):
                        hit = s == tabs[u]
                        for b in range(3):
                            acc[u][b] = jnp.where(hit, values[b], acc[u][b])
                for u in range(group):
                    for b in range(3):
                        target[
                            pl.ds(base + u * PW + v * 16, 16),
                            b * n + h * 128 : b * n + (h + 1) * 128,
                        ] = acc[u][b]

    def place_all(used):
        for o in range(used):
            for b in range(3):
                for v in range(9):
                    start = ((16 * v) % 9) * obs + o
                    for h in range(n // 128):
                        for tight, wide in ((tw, sw), (tz, sz)):
                            wide[h * 3 * obs + o * 3 + b, v * 16 : (v + 1) * 16, :] = tight[
                                h * 3 + b, pl.ds(start, 16, stride=obs), :
                            ].astype(BF)

        def place_w(i, c):
            if used == obs:
                place_one(sw, wp, i, i)
            else:
                place(sw, wp, i * 4, i * 4, 4, used)
            return c

        lax.fori_loop(0, SHOTS // PANEL // (1 if used == obs else 4), place_w, 0)
        group = min(4, panels)

        def place_z(i, c):
            place(sz, zp, i * group, i * group + first_panel, group, used)
            return c

        lax.fori_loop(0, panels // group, place_z, 0)

    pl.when(t < home_steps)(lambda: place_all(obs))
    pl.when(t >= home_steps)(lambda: place_all(2))

    def multiply(j, c):
        at = pl.ds(pl.multiple_of(j * 256, 256), 256)
        out_ref[:, at] += lax.dot_general(zp[...], wp[at, :], NT, preferred_element_type=F32)
        return c

    lax.fori_loop(0, columns // 256, multiply, 0)

    def multiply_own(q, c):
        at = pl.ds(pl.multiple_of(q * PW, PW), PW)
        dacc[at, 0:PW] += lax.dot_general(
            zp[at, :],
            wp[pl.ds(pl.multiple_of((q + first_panel) * PW, PW), PW), :],
            NT,
            preferred_element_type=F32,
        )
        return c

    lax.fori_loop(0, panels, multiply_own, 0)

    @pl.when(t == pl.num_programs(0) - 1)
    def _():
        acc = accu[...]
        for a in range(9):
            ut[pl.ds(a, share, stride=9), :] = acc if a == 0 else pltpu.roll(acc, 128 - 9 * a, 1)
            gt[pl.ds(a, share, stride=9), :] = pltpu.roll(acc, 128 - 81 - a, 1)
        u = ut[...] + damp_ref[...]
        high = u.astype(BF)
        low = (u - high.astype(F32)).astype(BF)
        rowcam = rowcam_ref[:, 0:1]

        def blocks(pick):
            return jnp.dot(high, pick, preferred_element_type=F32) + jnp.dot(
                low, pick, preferred_element_type=F32
            )

        def finish(j, c):
            at = pl.ds(pl.multiple_of(j * 256, 256), 256)
            hit = rowcam + first.astype(F32) == colcam_ref[0:1, at]
            out_ref[:, at] = jnp.where(hit, blocks(pick_ref[:, at]), 0.0) - out_ref[:, at]
            return c

        lax.fori_loop(0, columns // 256, finish, 0)
        local = rowcam_ref[:, 1:2]
        lane = lax.broadcasted_iota(jnp.int32, (rows, 256), 1)
        m = jnp.where(local == colcam_ref[0:1, 0:256], blocks(pick_ref[:, 0:256]), 0.0) - dacc[...]
        dacc[...] = jnp.where(lane == PW, gt[:, 0:1], m)

        def eliminate(half, k, c):
            for q in range(panels):
                at = slice(q * PW, (q + 1) * PW)
                ids = lax.broadcasted_iota(jnp.int32, (PW, 128), 1) + half * 128
                col = jnp.sum(
                    jnp.where(ids == k, dacc[at, half * 128 : (half + 1) * 128], 0.0),
                    axis=1,
                    keepdims=True,
                )
                pivot = dacc[pl.ds(q * PW + k, 1), :]
                wide = lax.broadcasted_iota(jnp.int32, (1, 256), 1)
                p = jnp.sum(jnp.where(wide == k, pivot, 0.0), axis=1, keepdims=True)
                scaled = pivot / p
                down = lax.broadcasted_iota(jnp.int32, (PW, 1), 0)
                col = jnp.where(down == k, 0.0, col)
                dacc[at, :] = dacc[at, :] - col * scaled
            return c

        lax.fori_loop(0, 128, functools.partial(eliminate, 0), 0)
        lax.fori_loop(128, PW, functools.partial(eliminate, 1), 0)
        for q in range(panels):
            at = slice(q * PW, (q + 1) * PW)
            m = dacc[at, :]
            down = lax.broadcasted_iota(jnp.int32, (PW, 256), 0)
            across = lax.broadcasted_iota(jnp.int32, (PW, 256), 1)
            diag = jnp.sum(jnp.where(down == across, m, 0.0), axis=1, keepdims=True)
            rhs = jnp.sum(jnp.where(across == PW, m, 0.0), axis=1, keepdims=True)
            step_ref[at, :] = jnp.broadcast_to(-(rhs / diag), (PW, 128))


def per_device(cam_jac, point_jac, residuals, obs_camera, obs_count, new_cluster, new_slot):
    clusters = lax.axis_size("cluster")
    members = lax.axis_size("member")
    me = lax.axis_index("cluster").astype(jnp.int32)
    my_member = lax.axis_index("member").astype(jnp.int32)
    obs, points = obs_camera.shape
    width = min(256, points)
    share = SHOTS // members
    rows = 9 * share
    columns = 9 * SHOTS
    vmem = pl.BlockSpec(memory_space=pltpu.VMEM)
    smem = pl.BlockSpec(memory_space=pltpu.SMEM)

    code = (new_cluster * SHOTS + new_slot).astype(F32)
    table = lax.dynamic_slice_in_dim(code, me * SHOTS, SHOTS, 0)[:, None]
    home, far = pl.pallas_call(
        functools.partial(pack_kernel, clusters=clusters, width=width),
        out_shape=(
            jax.ShapeDtypeStruct((points // width, ROWS, obs, width), BF),
            jax.ShapeDtypeStruct((clusters * BCAP, 64), BF),
        ),
        in_specs=[smem] + [vmem] * 6,
        out_specs=(vmem, vmem),
        scratch_shapes=[pltpu.VMEM((64, points), F32)],
        name="pack",
    )(me[None], table, cam_jac, point_jac, residuals, obs_camera, obs_count[None, :])

    far = jnp.broadcast_to(
        far.reshape(clusters, 1, BCAP, 64), (clusters, members, BCAP, 64)
    ).reshape(clusters * members, BCAP, 64)
    far = lax.all_to_all(far, ("cluster", "member"), split_axis=0, concat_axis=0, tiled=True)
    home = lax.all_to_all(
        jnp.broadcast_to(home[None], (members,) + home.shape),
        "member", split_axis=0, concat_axis=0, tiled=True,
    ).reshape(-1, ROWS, obs, width)
    far = far.reshape(-1, width, 2, 32)[:, :, :, :ROWS].transpose(0, 3, 2, 1)
    far = jnp.pad(far, ((0, 0), (0, 0), (0, obs - 2), (0, 0)))
    data = jnp.concatenate([home, far], axis=0)

    r = np.arange(rows)
    c = np.arange(columns)
    lane = np.arange(128)
    tab = jnp.asarray(np.broadcast_to((np.arange(PW) // 9)[:, None], (PW, 128)), BF)
    pick = jnp.asarray(lane[:, None] == c[None, :] % 9, BF)
    damp = jnp.asarray(DAMPING * (lane[None, :] == (r % 9)[:, None]), F32)
    rowcam = np.zeros((rows, 128), np.float32)
    rowcam[:, 0] = r // 9
    rowcam[:, 1] = (r // 9) % PANEL
    colcam = jnp.asarray(np.broadcast_to((c // 9)[None, :], (8, columns)), F32)
    full = lambda s: pl.BlockSpec(s, lambda t: (0,) * len(s))
    out, step = pl.pallas_call(
        functools.partial(main_kernel, share=share, home_steps=home.shape[0]),
        grid=(data.shape[0],),
        out_shape=(
            jax.ShapeDtypeStruct((rows, columns), F32),
            jax.ShapeDtypeStruct((rows, 128), F32),
        ),
        in_specs=[
            smem,
            pl.BlockSpec((1, ROWS, obs, width), lambda t: (t, 0, 0, 0)),
            full((PW, 128)),
            full((128, columns)),
            full((rows, 128)),
            full((rows, 128)),
            full((8, columns)),
        ],
        out_specs=(full((rows, columns)), full((rows, 128))),
        scratch_shapes=[
            pltpu.VMEM((width // 128 * 3, 24 * obs, 128), F32),
            pltpu.VMEM((width // 128 * 3, 24 * obs, 128), F32),
            pltpu.VMEM((width // 128, 128 * obs, 128), F32),
            pltpu.VMEM((width // 128 * 3 * obs, PW, 128), BF),
            pltpu.VMEM((width // 128 * 3 * obs, PW, 128), BF),
            pltpu.VMEM((width // 128 * obs, 16, 128), BF),
            pltpu.VMEM((columns, 3 * width), BF),
            pltpu.VMEM((rows, 3 * width), BF),
            pltpu.VMEM((share, 128), F32),
            pltpu.VMEM((rows, 128), F32),
            pltpu.VMEM((rows, 128), F32),
            pltpu.VMEM((rows, 256), F32),
        ],
        compiler_params=pltpu.CompilerParams(vmem_limit_bytes=56 * 1024 * 1024),
        name="schur",
    )((my_member * share)[None], data, tab, pick, damp, jnp.asarray(rowcam), colcam)
    return (out, step[:, 0])


def solution(mesh):
    in_specs = (
        P(None, None, ("cluster", "member")),
        P(None, None, ("cluster", "member")),
        P(None, None, ("cluster", "member")),
        P(None, ("cluster", "member")),
        P(("cluster", "member")),
        P(),
        P(),
    )
    out_specs = (P(("cluster", "member"), None), P(("cluster", "member")))
    return jax.shard_map(
        per_device, mesh=mesh, in_specs=in_specs, out_specs=out_specs, check_vma=False
    )
```
